32 devices in a mesh: expert: 4 (over z), seq: 4 (over y, x), dp: 2 (over core).
Axes of the slice: x: 2, y: 2, z: 4, core: 2. Of those that a mesh axis runs over, the one named last changes fastest.
Arguments:
- grad_out: bfloat16 [8, 512, 2048], P(('expert', 'dp'), 'seq'), may hold values from -6 to 6
- expert_ids: int32 [8, 512, 2], P(('expert', 'dp'), 'seq'), may hold values from 0 to 3, all different within a row; in each aligned block of 128 rows (0 to 127, 128 to 255, ..., all dimensions but the last counted through in order) at most 112 rows name the same one
- gate_weights: float32 [8, 512, 2], P(('expert', 'dp'), 'seq'), may hold values from 0.1 to 0.9
- hidden: bfloat16 [8, 512, 2, 7168], P(('expert', 'dp'), 'seq'), may hold values from -0.3125 to 0.3125
- queries: bfloat16 [8, 512, 2048], P(('expert', 'dp'), 'seq')
- keys: bfloat16 [8, 512, 512], P(('expert', 'dp'), 'seq')
- values: bfloat16 [8, 512, 512], P(('expert', 'dp'), 'seq'), may hold values from -6 to 6
Outputs:
- expert_grad: bfloat16 [4, 7168, 2048], P('expert', ('seq', 'dp'))
- grad_queries: bfloat16 [8, 512, 2048], P(('expert', 'dp'), 'seq')
- grad_keys: bfloat16 [8, 512, 512], P(('expert', 'dp'), 'seq')
- grad_values: bfloat16 [8, 512, 512], P(('expert', 'dp'), 'seq')
The draws below stay inside these ranges and needn't reach their ends.
Inputs may be any that keep to these rules, and one draw needn't show every extreme that they name: `expert_ids`: each position names two different experts; among the 128 positions of one device no expert is named more than 112 times.
All inputs are finite; a program needn't handle non-finite values.
Results may differ from the reference program's by a relative error of at most 0.018.
Values may be sent and summed in bfloat16 or wider, within the bound.
A program may use at most 128 MiB of HBM per device.

```python
import math
import jax
import jax.numpy as jnp
import numpy as np
from jax import lax

D = 2048
FF = 7168
HEADS = 16
KV_HEADS = 4
HEAD_DIM = 128
TOK_DEV = 128
LENGTH = 512
BATCH = 8
EXPERTS = 4
CAP = 112
N_SEQ = 4
N_DP = 2


def drawn_pair(key):
    queries = jax.random.normal(jax.random.fold_in(key, 101), (BATCH, LENGTH, HEADS * HEAD_DIM), jnp.float32)
    keys = jax.random.normal(jax.random.fold_in(key, 202), (BATCH, LENGTH, KV_HEADS, HEAD_DIM), jnp.float32)
    return (queries, keys.reshape(BATCH, LENGTH, KV_HEADS * HEAD_DIM))


def draw_queries(key, part):
    return drawn_pair(key)[0].astype(jnp.bfloat16)


def draw_keys(key, part):
    return drawn_pair(key)[1].astype(jnp.bfloat16)


def spiked(drawn, key, source, target, blocks, factor):
    def block_of(axis_at):
        return (jnp.arange(drawn.shape[axis_at]) // (drawn.shape[axis_at] // blocks)).reshape((-1,) + (1,) * (drawn.ndim - 1 - axis_at))

    one_side = jax.random.permutation(key, blocks)[block_of(target)]
    other_side = (block_of(target) + blocks // 2) % blocks
    return jnp.where((block_of(source) == one_side) | (block_of(source) == other_side), factor * drawn, drawn)


def levels(rng, dims, pieces, low, largest):
    def one(dim, parts):
        steps = jax.random.uniform(jax.random.fold_in(jax.random.fold_in(rng, 6), dim), (parts,), jnp.float32, low / len(pieces), largest / len(pieces))
        return jnp.repeat(jnp.exp(steps), dims[dim] // parts).reshape((-1,) + (1,) * (len(dims) - dim - 1))

    loudness = one(*pieces[0])
    for cut in pieces[1:]:
        loudness = loudness * one(*cut)
    return loudness


def assign_block(own_key, own, number, rows, number_of, top, reach, lean):
    ranking = jax.random.permutation(own_key, number_of)
    heavy_load, common = portions_of(number_of, rows * top, reach, lean, True), portions_of(number_of, rows * top, reach, lean, False)
    places = jnp.arange(number_of)

    def named(lengths, rotation):
        used = int((lengths > 0).sum())
        fixed = max(1, used // 4)
        shifted = fixed + (places - fixed + rotation * (used - fixed)) % max(1, number_of - fixed)
        return jnp.zeros((number_of,), jnp.int32).at[ranking[jnp.where(places < fixed, places, shifted)]].set(jnp.asarray(lengths, jnp.int32))

    lengths = jnp.where(number % 4 == 0, named(heavy_load, number // 4), named(common, number - number // 4 - 1))
    mixed = jax.random.permutation(jax.random.fold_in(own, 3), number_of)
    source_of, taker = mixed[0:number_of // 2 * 2:2], mixed[1:number_of // 2 * 2:2]
    slack = jnp.minimum(lengths[source_of] - 1, reach - lengths[taker]) // 2
    slack = jnp.where((source_of == ranking[0]) | (taker == ranking[0]) | (lengths[taker] == 0), 0, jnp.maximum(slack, 0))
    shifted = jax.random.randint(jax.random.fold_in(own, 4), (number_of // 2,), 0, 1 << 20) % (slack + 1)
    lengths = lengths.at[source_of].add(-shifted).at[taker].add(shifted)
    items = jnp.searchsorted(jnp.cumsum(lengths), jnp.arange(rows * top), side="right").astype(jnp.int32)
    table = items.reshape(top, rows).T
    table = table[jax.random.permutation(jax.random.fold_in(own, 1), rows)]
    rotation = jax.random.randint(jax.random.fold_in(own, 2), (rows, 1), 0, top)
    return jnp.take_along_axis(table, (jnp.arange(top)[None, :] + rotation) % top, axis=1)


def portions_of(count, total, reach, skew, full):
    weights = [(1 << 20) // math.isqrt(rank ** skew) + 1 for rank in range(1, count + 1)]
    largest = reach if full else min(reach, max(-(-total // count), total * weights[0] // sum(weights)))
    least = 1 if total - largest >= count - 1 else 0
    given, rest = [largest] + [least] * (count - 1), total - largest - least * (count - 1)
    while rest > 0:
        movable = [i for i in range(1, count) if given[i] < largest] or [i for i in range(1, count) if given[i] < reach]
        mass, budget = sum([weights[i] for i in movable]), rest
        for i in movable:
            more = min(reach - given[i], max(1, budget * weights[i] // mass), rest)
            given[i] = given[i] + more
            rest = rest - more
    return np.array(given)


def scatter_about(rng, dims, spread, limit, split=(), held_as=jnp.bfloat16):
    drawn = jax.random.normal(rng, dims, jnp.float32) * spread
    if len(split) > 0:
        drawn = levels(rng, dims, split, -0.22, 0.18) * drawn
    return jnp.clip(drawn, min=-limit, max=limit).astype(held_as)


def gaussian_with(key, shape, scale, reach, shards, heavy, held_as=jnp.bfloat16):
    result = scale * jax.random.normal(key, shape, jnp.float32)
    if shards:
        result = result * levels(key, shape, shards, -0.22, 0.18)
    return jnp.clip(spiked(result, jax.random.fold_in(key, 3), *heavy), -reach, reach).astype(held_as)


def setup_inputs(seed: int = 0) -> dict:
    streams_of = jax.random.split(jax.random.key(seed), 8)
    grad_out = scatter_about(streams_of[0], (BATCH, LENGTH, D), 1.0, 6.0, ((0, 8), (1, 4)))
    expert_ids_keys = jax.random.split(jax.random.fold_in(streams_of[1], 1), BATCH * LENGTH // TOK_DEV)
    expert_ids_turns = jax.random.permutation(jax.random.fold_in(streams_of[1], 3), BATCH * LENGTH // TOK_DEV)
    expert_ids = jax.vmap(lambda own, number: assign_block(jax.random.fold_in(streams_of[1], 2), own, number, TOK_DEV, EXPERTS, 2, CAP, 2))(expert_ids_keys, expert_ids_turns).reshape((BATCH, LENGTH, 2))
    gate_weights = jnp.clip(0.1 + 0.79999997 * jax.random.uniform(streams_of[2], (BATCH, LENGTH, 2), jnp.float32) ** levels(streams_of[2], (BATCH, LENGTH, 2), ((0, 8), (1, 4)), -0.2, 0.2), 0.1, 0.9)
    hidden = gaussian_with(streams_of[3], (BATCH, LENGTH, 2, FF), (0.5 * (N_DP * N_SEQ * TOK_DEV) ** -0.5), 0.3125, ((0, 8), (1, 4)), (0, 3, 8, 2.0))
    queries = draw_queries(jax.random.fold_in(streams_of[7], 71), 0)
    keys = draw_keys(jax.random.fold_in(streams_of[7], 71), 0)
    values = scatter_about(streams_of[6], (BATCH, LENGTH, KV_HEADS * HEAD_DIM), 1.0, 6.0, ((0, 8), (1, 4)))
    return {"grad_out": grad_out, "expert_ids": expert_ids, "gate_weights": gate_weights, "hidden": hidden, "queries": queries, "keys": keys, "values": values}


def expert_grads(grad_out, expert_ids, gate_weights, hidden):
    row_total = BATCH * LENGTH * 2
    flat_ids = expert_ids.reshape(row_total).astype(jnp.int32)
    scaled = (gate_weights[..., None] * grad_out[:, :, None, :].astype(jnp.float32)).astype(jnp.bfloat16)
    scaled = scaled.reshape(row_total, D)
    flat_hidden = hidden.reshape(row_total, FF)
    row_order = jnp.argsort(flat_ids, stable=True).astype(jnp.int32)
    onehot = (flat_ids[:, None] == jnp.arange(EXPERTS, dtype=jnp.int32)[None, :]).astype(jnp.int32)
    counts = jnp.sum(onehot, axis=0).astype(jnp.int32)
    starts = (jnp.cumsum(counts) - counts).astype(jnp.int32)
    most_rows = BATCH * N_SEQ * CAP
    padded = jnp.concatenate([row_order, jnp.zeros((most_rows,), jnp.int32)])

    def one_expert(expert):
        picked = lax.dynamic_slice(padded, (starts[expert],), (most_rows,))
        usable = jnp.arange(most_rows, dtype=jnp.int32) < counts[expert]
        picked_hidden = jnp.where(usable[:, None], flat_hidden[picked], jnp.zeros((), jnp.bfloat16))
        picked_scaled = jnp.where(usable[:, None], scaled[picked], jnp.zeros((), jnp.bfloat16))
        total = jnp.dot(picked_hidden.T, picked_scaled, preferred_element_type=jnp.float32)
        return total.astype(jnp.bfloat16)

    return lax.map(one_expert, jnp.arange(EXPERTS, dtype=jnp.int32))


def attention_grads(queries, keys, values, grad_out):
    per_group = HEADS // KV_HEADS
    score_scale = HEAD_DIM ** -0.5

    def one_sequence(operands):
        query_rows, key_rows, value_rows, out_rows = operands
        query_heads = query_rows.astype(jnp.float32).reshape(LENGTH, KV_HEADS, per_group, HEAD_DIM)
        out_heads = out_rows.astype(jnp.float32).reshape(LENGTH, KV_HEADS, per_group, HEAD_DIM)
        key_heads = key_rows.astype(jnp.float32).reshape(LENGTH, KV_HEADS, HEAD_DIM)
        value_heads = value_rows.astype(jnp.float32).reshape(LENGTH, KV_HEADS, HEAD_DIM)
        scores = jnp.einsum("qhgd,khd->hgqk", query_heads, key_heads) * score_scale
        row_max = jnp.max(scores, axis=-1, keepdims=True)
        raised = jnp.exp(scores - row_max)
        probabilities = raised / jnp.sum(raised, axis=-1, keepdims=True)
        probs_low = probabilities.astype(jnp.bfloat16)
        dprobs = jnp.einsum("qhgd,khd->hgqk", out_heads, value_heads)
        row_delta = jnp.sum(probabilities * dprobs, axis=-1, keepdims=True)
        dscores = (probabilities * (dprobs - row_delta)).astype(jnp.bfloat16)
        grad_v = jnp.einsum("hgqk,qhgd->khd", probs_low.astype(jnp.float32), out_heads)
        grad_q = jnp.einsum("hgqk,khd->qhgd", dscores.astype(jnp.float32), key_heads) * score_scale
        grad_k = jnp.einsum("hgqk,qhgd->khd", dscores.astype(jnp.float32), query_heads) * score_scale
        return (grad_q.reshape(LENGTH, HEADS * HEAD_DIM).astype(jnp.bfloat16),
                grad_k.reshape(LENGTH, KV_HEADS * HEAD_DIM).astype(jnp.bfloat16),
                grad_v.reshape(LENGTH, KV_HEADS * HEAD_DIM).astype(jnp.bfloat16))

    return lax.map(one_sequence, (queries, keys, values, grad_out))


def reference(grad_out, expert_ids, gate_weights, hidden, queries, keys, values):
    expert_grad = expert_grads(grad_out, expert_ids, gate_weights, hidden)
    grad_queries, grad_keys, grad_values = attention_grads(queries, keys, values, grad_out)
    return (expert_grad, grad_queries, grad_keys, grad_values)
```

```python
import functools

import jax
import jax.numpy as jnp
from jax import lax
from jax.experimental import pallas as pl
from jax.experimental.pallas import tpu as pltpu
from jax.sharding import PartitionSpec as P

HEADS = 16
KV_HEADS = 4
HEAD_DIM = 128
GROUP = HEADS // KV_HEADS
MESH = pl.DeviceIdType.MESH


def dot(a, b, contract):
    return lax.dot_general(a, b, (contract, ((), ())), preferred_element_type=jnp.float32)


def routing_codes(ids, order_row, order_col, experts, capacity):
    count = max(8, experts)
    rows = ids.shape[1]
    expert_of = lax.broadcasted_iota(jnp.int32, (count, rows), 0).astype(jnp.float32)
    onehot = (expert_of == ids).astype(jnp.float32)
    earlier = (order_col < order_row).astype(jnp.float32)
    before = dot(onehot.astype(jnp.bfloat16), earlier.astype(jnp.bfloat16), ((1,), (0,)))
    slot = jnp.sum(before * onehot, axis=0, keepdims=True)
    return ids * float(capacity) + slot


def kernel(
    dims,
    ids_t, ids_k, gates_k, go, q, k, v, hid,
    eg_out, gq_out, gk_out, gv_out,
    kbuf, vbuf, idbuf, hraw, hsend, hrecv, gsend, grecv,
    kpart, vpart, kown, vown, kin, vin, precv,
    small_send, small_recv, local_sem, hraw_send, hraw_recv,
    gz_send, gz_recv, gs_send, gs_recv, hz_send, hz_recv,
    part_send, part_recv, pair_send, pair_recv,
):
    E, S, T, C, U, D = dims
    half = U // 2
    e = lax.axis_index("expert")
    s = lax.axis_index("seq")
    d = lax.axis_index("dp")
    seq_peer = [lax.rem(s + i, S) for i in range(S)]

    def ex_peer(j):
        return lax.rem(e + j, E)

    barrier = pltpu.get_barrier_semaphore()
    for i in range(1, S):
        pl.semaphore_signal(barrier, inc=1, device_id={"seq": seq_peer[i]}, device_id_type=MESH)

    @pl.loop(1, E)
    def _(j):
        pl.semaphore_signal(barrier, inc=1, device_id={"expert": ex_peer(j)}, device_id_type=MESH)

    pl.semaphore_signal(barrier, inc=1, device_id={"dp": 1 - d}, device_id_type=MESH)
    pl.semaphore_wait(barrier, S + E - 1)

    def send(src, dst, ssem, rsem, where):
        return pltpu.make_async_remote_copy(
            src_ref=src, dst_ref=dst, send_sem=ssem, recv_sem=rsem,
            device_id=where, device_id_type=MESH,
        )

    def small_copy(n, i, slot):
        src, dst = ((ids_t, idbuf), (k, kbuf), (v, vbuf))[n]
        return send(src, dst.at[slot], small_send.at[n, i], small_recv.at[n, slot], {"seq": seq_peer[i]})

    def raw_copy(i, slot):
        cols = pl.ds(pl.multiple_of(seq_peer[i] * U, 128), U)
        return send(hid.at[:, cols], hraw.at[slot], hraw_send.at[i], hraw_recv.at[slot], {"seq": seq_peer[i]})

    own_cols = pl.ds(pl.multiple_of(s * U, 128), U)
    own_raw = pltpu.make_async_copy(hid.at[:, own_cols], hraw.at[s], local_sem.at[0])
    own_raw.start()
    for i in range(1, S):
        for n in range(3):
            small_copy(n, i, s).start()
    for i in range(1, S):
        raw_copy(i, s).start()
    kbuf[s] = k[...]
    vbuf[s] = v[...]
    idbuf[s] = ids_t[...]

    rows = 2 * T
    col = lax.broadcasted_iota(jnp.int32, (rows, rows), 1)
    row = lax.broadcasted_iota(jnp.int32, (rows, rows), 0)
    code = routing_codes(
        ids_k[0:1, :], 2 * lax.rem(col, T) + col // T, 2 * lax.rem(row, T) + row // T, E, C
    )
    place = lax.broadcasted_iota(jnp.int32, (E * C, rows), 0).astype(jnp.float32)
    picks = (place == code).astype(jnp.float32)
    gate = jnp.sum(picks * gates_k[0:1, :], axis=1, keepdims=True)
    token_picks = (picks[:, :T] + picks[:, T:]).astype(jnp.bfloat16)
    gsend[...] = (dot(token_picks, go[...], ((1,), (0,))) * gate).astype(jnp.bfloat16)

    def expert_rows(p):
        return pl.ds(pl.multiple_of(p * C, 16), C)

    def gz_copy(j, slot):
        p = ex_peer(j)
        return send(gsend.at[expert_rows(p)], grecv.at[s, slot], gz_send.at[j], gz_recv.at[slot], {"expert": p})

    def gs_copy(i, z, slot):
        return send(grecv.at[s, z], grecv.at[slot, z], gs_send.at[i, z], gs_recv.at[slot, z], {"seq": seq_peer[i]})

    def gs_wait(i, z):
        slot = seq_peer[i]
        send(grecv.at[s, z], grecv.at[slot, z], gs_send.at[i, z], gs_recv.at[slot, z], {"seq": slot}).wait_recv()

    @pl.loop(1, E)
    def _(j):
        gz_copy(j, e).start()

    grecv[s, e] = gsend[expert_rows(e)]
    for i in range(1, S):
        gs_copy(i, e, s).start()

    def hz_copy(i, j, slot):
        p = ex_peer(j)
        src = seq_peer[i]
        return send(hsend.at[src, expert_rows(p)], hrecv.at[src, slot], hz_send.at[src, j], hz_recv.at[src, slot], {"expert": p})

    def pack_hidden(i):
        src = seq_peer[i]
        hcode = routing_codes(idbuf[src, 0:1, :], col, row, E, C)
        hpicks = (place == hcode).astype(jnp.bfloat16)
        for u0 in range(0, U, half):
            hsend[src, :, u0 : u0 + half] = dot(
                hpicks, hraw[src, :, u0 : u0 + half], ((1,), (0,))
            ).astype(jnp.bfloat16)

        @pl.loop(1, E)
        def _(j):
            hz_copy(i, j, e).start()

        hrecv[src, e] = hsend[src, expert_rows(e)]

    own_raw.wait()
    pack_hidden(0)

    scale = HEAD_DIM ** (-0.5)
    length = S * T

    def attention(j):
        lanes = slice(j * HEAD_DIM, (j + 1) * HEAD_DIM)
        heads = [slice(h * HEAD_DIM, (h + 1) * HEAD_DIM) for h in range(j * GROUP, (j + 1) * GROUP)]
        qs = jnp.concatenate([q[:, h] for h in heads], axis=0)
        gs = jnp.concatenate([go[:, h] for h in heads], axis=0)
        kj = kbuf[:, :, lanes].reshape(length, HEAD_DIM)
        vj = vbuf[:, :, lanes].reshape(length, HEAD_DIM)
        scores = dot(qs, kj, ((1,), (1,))) * scale
        raised = jnp.exp(scores - jnp.max(scores, axis=-1, keepdims=True))
        probs = raised / jnp.sum(raised, axis=-1, keepdims=True)
        dprobs = dot(gs, vj, ((1,), (1,)))
        delta = jnp.sum(probs * dprobs, axis=-1, keepdims=True)
        ds = (probs * (dprobs - delta)).astype(jnp.bfloat16)
        dv = dot(probs.astype(jnp.bfloat16), gs, ((0,), (0,)))
        dk = dot(ds, qs, ((0,), (0,))) * scale
        dq = dot(ds, kj, ((1,), (0,))) * scale
        for n, h in enumerate(heads):
            gq_out[:, h] = dq[n * T : (n + 1) * T].astype(jnp.bfloat16)
        dk = dk.reshape(S, T, HEAD_DIM)
        dv = dv.reshape(S, T, HEAD_DIM)
        kown[:, :, lanes] = dk
        vown[:, :, lanes] = dv
        kpart[:, :, lanes] = dk.astype(jnp.bfloat16)
        vpart[:, :, lanes] = dv.astype(jnp.bfloat16)

    for i in range(1, S):
        for n in range(3):
            small_copy(n, i, seq_peer[i]).wait_recv()

    attention(0)

    @pl.loop(1, E)
    def _(j):
        z = ex_peer(j)
        gz_copy(j, z).wait_recv()
        for i in range(1, S):
            gs_copy(i, z, s).start()

    attention(1)
    for i in range(1, S):
        raw_copy(i, seq_peer[i]).wait_recv()
        pack_hidden(i)
        if i + 1 < KV_HEADS:
            attention(i + 1)
    for j in range(S, KV_HEADS):
        attention(j)

    def part_copy(n, i, slot):
        src, dst = ((kpart, kin), (vpart, vin))[n]
        return send(src.at[seq_peer[i]], dst.at[slot], part_send.at[n, i], part_recv.at[n, slot], {"seq": seq_peer[i]})

    for i in range(1, S):
        for n in range(2):
            part_copy(n, i, s).start()
    for n, (own, got, out) in enumerate(((kown, kin, gk_out), (vown, vin, gv_out))):
        total = own[s]
        for i in range(1, S):
            part_copy(n, i, seq_peer[i]).wait_recv()
            total = total + got[seq_peer[i]].astype(jnp.float32)
        out[...] = total.astype(jnp.bfloat16)

    @pl.loop(1, E)
    def _(j):
        for i in range(S):
            hz_copy(i, j, ex_peer(j)).wait_recv()

    @pl.loop(0, E)
    def _(z):
        for i in range(1, S):
            gs_wait(i, z)

    wide = 256
    tiles = [(o, min(wide, half - o)) for o in range(0, half, wide)]

    def product(base, off, width):
        units = pl.ds(pl.multiple_of(base + off, 128), width)
        h = hrecv[:, :, :, units].reshape(S * E * C, width)
        return dot(h, grecv[...].reshape(S * E * C, D), ((0,), (0,)))

    def pair_copy(n):
        off, width = tiles[n]
        return send(eg_out.at[off : off + width], precv.at[off : off + width], pair_send.at[n], pair_recv.at[n], {"dp": 1 - d})

    for n, (off, width) in enumerate(tiles):
        eg_out[off : off + width, :] = product((1 - d) * half, off, width).astype(jnp.bfloat16)
        pair_copy(n).start()
    for n, (off, width) in enumerate(tiles):
        mine = product(d * half, off, width)
        pair_copy(n).wait_recv()
        pair_copy(n).wait_send()
        got = precv[off : off + width, :].astype(jnp.float32)
        eg_out[off : off + width, :] = (mine + got).astype(jnp.bfloat16)

    for i in range(1, S):
        for n in range(3):
            small_copy(n, i, s).wait_send()
        for n in range(2):
            part_copy(n, i, s).wait_send()
        raw_copy(i, s).wait_send()

    @pl.loop(0, E)
    def _(z):
        for i in range(1, S):
            gs_copy(i, z, s).wait_send()

    @pl.loop(1, E)
    def _(j):
        gz_copy(j, e).wait_send()
        for i in range(S):
            hz_copy(i, j, e).wait_send()


def on_device(grad_out, expert_ids, gate_weights, hidden, queries, keys, values):
    E = lax.axis_size("expert")
    S = lax.axis_size("seq")
    T = grad_out.shape[1]
    D = grad_out.shape[2]
    U = hidden.shape[3] // S
    C = -(-(7 * T // (2 * E)) // 16) * 16
    KD = keys.shape[2]
    rows = 2 * T
    bf, f32 = jnp.bfloat16, jnp.float32
    ids = expert_ids[0].astype(f32)
    ids_t = jnp.broadcast_to(ids.reshape(1, rows), (8, rows))
    ids_k = jnp.broadcast_to(ids.T.reshape(1, rows), (8, rows))
    gates_k = jnp.broadcast_to(gate_weights[0].T.reshape(1, rows), (8, rows))
    tiles = -(-(U // 2) // 256)
    vm = pl.BlockSpec(memory_space=pltpu.VMEM)
    dma = pltpu.SemaphoreType.DMA
    eg, gq, gk, gv = pl.pallas_call(
        functools.partial(kernel, (E, S, T, C, U, D)),
        out_shape=(
            jax.ShapeDtypeStruct((U // 2, D), bf),
            jax.ShapeDtypeStruct((T, queries.shape[2]), bf),
            jax.ShapeDtypeStruct((T, KD), bf),
            jax.ShapeDtypeStruct((T, KD), bf),
        ),
        in_specs=[vm] * 7 + [pl.BlockSpec(memory_space=pl.ANY)],
        out_specs=(vm,) * 4,
        scratch_shapes=[
            pltpu.VMEM((S, T, KD), bf),
            pltpu.VMEM((S, T, KD), bf),
            pltpu.VMEM((S, 8, rows), f32),
            pltpu.VMEM((S, rows, U), bf),
            pltpu.VMEM((S, E * C, U), bf),
            pltpu.VMEM((S, E, C, U), bf),
            pltpu.VMEM((E * C, D), bf),
            pltpu.VMEM((S, E, C, D), bf),
            pltpu.VMEM((S, T, KD), bf),
            pltpu.VMEM((S, T, KD), bf),
            pltpu.VMEM((S, T, KD), f32),
            pltpu.VMEM((S, T, KD), f32),
            pltpu.VMEM((S, T, KD), bf),
            pltpu.VMEM((S, T, KD), bf),
            pltpu.VMEM((U // 2, D), bf),
            dma((3, S)), dma((3, S)), dma((1,)), dma((S,)), dma((S,)),
            dma((E,)), dma((E,)), dma((S, E)), dma((S, E)), dma((S, E)), dma((S, E)),
            dma((2, S)), dma((2, S)), dma((tiles,)), dma((tiles,)),
        ],
        compiler_params=pltpu.CompilerParams(
            collective_id=0, has_side_effects=True, vmem_limit_bytes=60 * 1024 * 1024
        ),
    )(ids_t, ids_k, gates_k, grad_out[0], queries[0], keys[0], values[0], hidden.reshape(rows, S * U))
    return (eg[None], gq[None], gk[None], gv[None])


def solution(mesh):
    split = P(("expert", "dp"), "seq", None)
    in_specs = (split, split, split, P(("expert", "dp"), "seq", None, None), split, split, split)
    out_specs = (P("expert", ("seq", "dp"), None), split, split, split)
    return jax.shard_map(
        on_device, mesh=mesh, in_specs=in_specs, out_specs=out_specs, check_vma=False
    )
```
